32 devices in a mesh: group: 2 (over x), expert: 16 (over z, y, core).
Axes of the slice: x: 2, y: 2, z: 4, core: 2. Of those that a mesh axis runs over, the one named last changes fastest.
Arguments:
- tokens: bfloat16 [16, 16, 2048], P('expert', 'group'), may hold values from -6 to 6
- out_grad: bfloat16 [16, 16, 2048], P('expert', 'group'), may hold values from -6 to 6
- gates: bfloat16 [16, 16, 8], P('expert', 'group'), may hold values from 0.049804688 to 0.34960938
- routes: int32 [16, 16, 8], P('expert', 'group'), may hold values from 0 to 31, as said below
- shard_of: int32 [2, 16], replicated, may hold values from 0 to 15, each once within a row
- w_gate: bfloat16 [2, 16, 768, 2048], P('group', 'expert'), may hold values from -0.125 to 0.125
- w_up: bfloat16 [2, 16, 768, 2048], P('group', 'expert'), may hold values from -0.125 to 0.125
- w_down: bfloat16 [2, 16, 768, 2048], P('group', 'expert'), may hold values from -0.21875 to 0.21875
Outputs:
- input_grad: bfloat16 [16, 16, 2048], P('expert', 'group')
- routing_grad: float32 [16, 16, 8], P('expert', 'group')
- gate_weight_grad: bfloat16 [2, 16, 768, 2048], P('group', 'expert')
- up_weight_grad: bfloat16 [2, 16, 768, 2048], P('group', 'expert')
- down_weight_grad: bfloat16 [2, 16, 768, 2048], P('group', 'expert')
The draws below stay inside these ranges and needn't reach their ends.
Inputs may be any that keep to these rules, and one draw needn't show every extreme that they name: Each token names 8 different experts. Among the 16 tokens routes[p] of one position p, each expert is named at most 8 times, and one expert is named exactly 8 times at every position. `shard_of`: each row is a permutation of the device positions' shard numbers.
All inputs are finite; a program needn't handle non-finite values.
Results may differ from the reference program's by a relative error of at most 0.0058.
Values may be sent and summed in bfloat16 or wider, within the bound.
No kernel may reach another device: no remote copies, remote signals or barrier semaphores. Data moves between devices by JAX's collectives and lax.ppermute only.
A program may use at most 64 MiB of HBM per device.

```python
import jax
import jax.numpy as jnp
from jax import lax

D = 2048
F = 768
EXP_GROUP = 16
TOP = 8
EXPERT_COUNT = 32
SHARDS = 1
FS = 768
BLOCK = 16
CAP = 8
N_GROUP = 2
N_EXPERT = 16


def draw_routes(key, part):
    popular_random_key, extra_random_key, blocks_random_key = jax.random.split(jax.random.fold_in(key, 11), 3)
    hot_expert = jax.random.randint(popular_random_key, (), 0, EXPERT_COUNT)
    extra_scores = jax.random.randint(extra_random_key, (EXPERT_COUNT,), 0, 4)
    slot_count = EXPERT_COUNT * CAP
    pair_count = BLOCK * TOP
    slot_expert = jnp.arange(slot_count, dtype=jnp.int32) // CAP
    slot_rank = jnp.arange(slot_count, dtype=jnp.int32) % CAP

    def one_block(block_key):
        score_key, order_key, rows_key = jax.random.split(block_key, 3)
        jitter = jax.random.randint(score_key, (slot_count,), 0, 1024)
        scores = jnp.where(slot_expert == hot_expert, 4096 + jitter, extra_scores[slot_expert] * 256 + jitter)
        scores = scores * slot_count + jnp.arange(slot_count, dtype=jnp.int32)
        ranking = jnp.argsort(-scores)
        chosen = jnp.zeros((slot_count,), jnp.int32).at[ranking[:pair_count]].set(1)
        expert_rank = jax.random.permutation(order_key, EXPERT_COUNT)
        sort_key = jnp.where(chosen == 1, expert_rank[slot_expert] * CAP + slot_rank, slot_count + jnp.arange(slot_count, dtype=jnp.int32))
        listed = slot_expert[jnp.argsort(sort_key)][:pair_count]
        expert_ids = listed.reshape(TOP, BLOCK).T
        row_order = jax.random.permutation(rows_key, BLOCK)
        return expert_ids[row_order]
    block_keys = jax.random.split(blocks_random_key, N_EXPERT)
    return jax.vmap(one_block)(block_keys).astype(jnp.int32)


def block_levels(own_key, dims, pieces, smallest, high):
    gain = 1.0
    for axis_at, blocks in pieces:
        steps = jax.random.uniform(jax.random.fold_in(jax.random.fold_in(own_key, 6), axis_at), (blocks,), jnp.float32, smallest / len(pieces), high / len(pieces))
        gain = gain * jnp.repeat(jnp.exp(steps), dims[axis_at] // blocks).reshape((-1,) + (1,) * (len(dims) - 1 - axis_at))
    return gain


def normal_values(own_key, extent, deviation, limit, cuts=(), held_as=jnp.bfloat16):
    factor_of = block_levels(own_key, extent, cuts, -0.22, 0.18) if cuts else 1.0
    drawn = jax.random.normal(own_key, extent, jnp.float32) * deviation * factor_of
    return jnp.minimum(jnp.maximum(drawn, -limit), limit).astype(held_as)


def setup_inputs(seed: int = 0) -> dict:
    key_of = jax.random.split(jax.random.key(seed), 9)
    tokens = normal_values(key_of[0], (N_EXPERT, BLOCK, D), 1.0, 6.0, ((0, 16), (1, 2)))
    out_grad = normal_values(key_of[1], (N_EXPERT, BLOCK, D), 1.0, 6.0, ((0, 16), (1, 2)))
    gates = jnp.clip(0.049804688 + 0.2998047 * jax.random.uniform(key_of[2], (N_EXPERT, BLOCK, TOP), jnp.float32) ** block_levels(key_of[2], (N_EXPERT, BLOCK, TOP), ((0, 16), (1, 2)), -0.2, 0.2), 0.049804688, 0.34960938).astype(jnp.bfloat16)
    routes = draw_routes(jax.random.fold_in(key_of[8], 71), 0)
    shard_of = jax.vmap(lambda own: jax.random.permutation(own, N_EXPERT))(jax.random.split(key_of[4], N_GROUP)).reshape((N_GROUP, N_EXPERT)).astype(jnp.int32)
    w_gate = normal_values(key_of[5], (N_GROUP, N_EXPERT, FS, D), D ** -0.5, 0.125, ((0, 2), (1, 16)))
    w_up = normal_values(key_of[6], (N_GROUP, N_EXPERT, FS, D), D ** -0.5, 0.125, ((0, 2), (1, 16)))
    w_down = normal_values(key_of[7], (N_GROUP, N_EXPERT, FS, D), F ** -0.5, 0.21875, ((0, 2), (1, 16)))
    return {"tokens": tokens, "out_grad": out_grad, "gates": gates, "routes": routes, "shard_of": shard_of, "w_gate": w_gate, "w_up": w_up, "w_down": w_down}


def expert_backward(rows_in, rows_grad, row_gates, gate_shard, up_shard, down_shard):
    contraction_dims = (((1,), (1,)), ((), ()))
    gate_pre = lax.dot_general(rows_in, gate_shard, contraction_dims, preferred_element_type=jnp.float32)
    up_pre = lax.dot_general(rows_in, up_shard, contraction_dims, preferred_element_type=jnp.float32)
    back_hidden = lax.dot_general(rows_grad, down_shard, contraction_dims, preferred_element_type=jnp.float32)
    sigmoid = jax.nn.sigmoid(gate_pre)
    swish_gate = gate_pre * sigmoid
    hidden = swish_gate * up_pre
    gate_part = jnp.sum(back_hidden * hidden, axis=1).astype(jnp.bfloat16)
    hidden_grad = row_gates[:, None] * back_hidden
    gate_grad = (hidden_grad * up_pre * sigmoid * (1.0 + gate_pre * (1.0 - sigmoid))).astype(jnp.bfloat16)
    up_grad = (hidden_grad * swish_gate).astype(jnp.bfloat16)
    input_part = (jnp.dot(gate_grad, gate_shard, preferred_element_type=jnp.float32) + jnp.dot(up_grad, up_shard, preferred_element_type=jnp.float32)).astype(jnp.bfloat16)
    gate_weighted = (row_gates[:, None] * hidden).astype(jnp.bfloat16)
    return input_part, gate_part, gate_grad, up_grad, gate_weighted


def weight_grads(rows_in, rows_grad, gate_grad, up_grad, gate_weighted):
    contraction_dims = (((0,), (0,)), ((), ()))
    first = lax.dot_general(gate_grad, rows_in, contraction_dims, preferred_element_type=jnp.float32).astype(jnp.bfloat16)
    second = lax.dot_general(up_grad, rows_in, contraction_dims, preferred_element_type=jnp.float32).astype(jnp.bfloat16)
    third = lax.dot_general(gate_weighted, rows_grad, contraction_dims, preferred_element_type=jnp.float32).astype(jnp.bfloat16)
    return first, second, third


def reference(tokens, out_grad, gates, routes, shard_of, w_gate, w_up, w_down):
    token_total = N_EXPERT * BLOCK
    flat_in = jnp.concatenate([tokens.reshape(token_total, D), jnp.zeros((1, D), jnp.bfloat16)], axis=0)
    flattened_gradient = jnp.concatenate([out_grad.reshape(token_total, D), jnp.zeros((1, D), jnp.bfloat16)], axis=0)
    flat_gates = jnp.concatenate([gates.reshape(token_total * TOP).astype(jnp.float32), jnp.zeros((1,), jnp.float32)], axis=0)
    expert_ids = routes.reshape(N_EXPERT, BLOCK * TOP)
    onehot = (expert_ids[:, :, None] == jnp.arange(EXPERT_COUNT, dtype=jnp.int32)[None, None, :]).astype(jnp.int32)
    slot_rank = jnp.sum((jnp.cumsum(onehot, axis=1) - 1) * onehot, axis=2).astype(jnp.int32)
    position = jnp.broadcast_to(jnp.arange(N_EXPERT, dtype=jnp.int32)[:, None], expert_ids.shape)
    pair_flat = jnp.arange(token_total * TOP, dtype=jnp.int32).reshape(N_EXPERT, BLOCK * TOP)
    token_flat = pair_flat // TOP
    token_table = jnp.full((EXPERT_COUNT, N_EXPERT, CAP), token_total, jnp.int32).at[expert_ids, position, slot_rank].set(token_flat)
    pair_table = jnp.full((EXPERT_COUNT, N_EXPERT, CAP), token_total * TOP, jnp.int32).at[expert_ids, position, slot_rank].set(pair_flat)
    device_ids = jnp.arange(N_GROUP * N_EXPERT, dtype=jnp.int32)
    experts_held = ((device_ids // N_EXPERT) * EXP_GROUP + shard_of.reshape(-1) // SHARDS).astype(jnp.int32)

    def visit(carry, inputs):
        input_acc, gate_acc = carry
        expert_now, gate_shard, up_shard, down_shard = inputs
        token_rows = token_table[expert_now].reshape(-1)
        pair_rows = pair_table[expert_now].reshape(-1)
        rows_in = flat_in[token_rows]
        rows_grad = flattened_gradient[token_rows]
        row_gates = flat_gates[pair_rows]
        input_part, gate_part, gate_grad, up_grad, gate_weighted = expert_backward(rows_in, rows_grad, row_gates, gate_shard, up_shard, down_shard)
        input_part, gate_part = lax.optimization_barrier((input_part, gate_part))
        input_acc = input_acc.at[token_rows].add(input_part.astype(jnp.float32))
        gate_acc = gate_acc.at[pair_rows].add(gate_part.astype(jnp.float32))
        return (input_acc, gate_acc), weight_grads(rows_in, rows_grad, gate_grad, up_grad, gate_weighted)

    start = (jnp.zeros((token_total + 1, D), jnp.float32), jnp.zeros((token_total * TOP + 1,), jnp.float32))
    scanned = (experts_held, w_gate.reshape(-1, FS, D), w_up.reshape(-1, FS, D), w_down.reshape(-1, FS, D))
    (input_acc, gate_acc), grads = lax.scan(visit, start, scanned)
    input_grad = input_acc[:token_total].reshape(N_EXPERT, BLOCK, D).astype(jnp.bfloat16)
    routing_grad = gate_acc[:token_total * TOP].reshape(N_EXPERT, BLOCK, TOP)
    shape_out = (N_GROUP, N_EXPERT, FS, D)
    return input_grad, routing_grad, grads[0].reshape(shape_out), grads[1].reshape(shape_out), grads[2].reshape(shape_out)
```

```python
import functools

import jax
import jax.numpy as jnp
from jax import lax
from jax.experimental import pallas as pl
from jax.experimental.pallas import tpu as pltpu
from jax.sharding import Mesh
from jax.sharding import PartitionSpec as P

EXP_GROUP = 16
CAP = 8
LANES = 128
F32 = jnp.float32
BF16 = jnp.bfloat16
VMEM_LIMIT = 56 * 1024 * 1024


def expert_backward(rows_in, rows_grad, row_gates, gate_shard, up_shard, down_shard):
    contraction_dims = (((1,), (1,)), ((), ()))
    gate_pre = lax.dot_general(rows_in, gate_shard, contraction_dims, preferred_element_type=F32)
    up_pre = lax.dot_general(rows_in, up_shard, contraction_dims, preferred_element_type=F32)
    back_hidden = lax.dot_general(
        rows_grad, down_shard, contraction_dims, preferred_element_type=F32
    )
    sigmoid = jax.nn.sigmoid(gate_pre)
    swish_gate = gate_pre * sigmoid
    hidden = swish_gate * up_pre
    gate_part = jnp.sum(back_hidden * hidden, axis=1).astype(BF16)
    hidden_grad = row_gates[:, None] * back_hidden
    gate_grad = (hidden_grad * up_pre * sigmoid * (1.0 + gate_pre * (1.0 - sigmoid))).astype(BF16)
    up_grad = (hidden_grad * swish_gate).astype(BF16)
    input_part = (
        jnp.dot(gate_grad, gate_shard, preferred_element_type=F32)
        + jnp.dot(up_grad, up_shard, preferred_element_type=F32)
    ).astype(BF16)
    gate_weighted = (row_gates[:, None] * hidden).astype(BF16)
    return (input_part, gate_part, gate_grad, up_grad, gate_weighted)


def weight_grads(rows_in, rows_grad, gate_grad, up_grad, gate_weighted):
    contraction_dims = (((0,), (0,)), ((), ()))

    def one(a, b):
        return lax.dot_general(a, b, contraction_dims, preferred_element_type=F32).astype(BF16)

    return one(gate_grad, rows_in), one(up_grad, rows_in), one(gate_weighted, rows_grad)


def exchange(x):
    return lax.all_to_all(x, "expert", split_axis=0, concat_axis=0, tiled=True)


def general_local(tokens, out_grad, gates, routes, shard_of, w_gate, w_up, w_down):
    positions = lax.axis_size("expert")
    group_now = lax.axis_index("group")
    shards = positions // EXP_GROUP
    gather = functools.partial(lax.all_gather, axis_name="group", axis=1, tiled=True)
    all_in, all_grad, all_gates, all_ids = (
        gather(tokens),
        gather(out_grad),
        gather(gates),
        gather(routes),
    )
    width = tokens.shape[2]
    block_rows = all_in.shape[1]
    top_k = routes.shape[2]
    pair_total = block_rows * top_k
    bucket_total = EXP_GROUP * CAP
    local_ids = all_ids.reshape(pair_total) - group_now * EXP_GROUP
    onehot = (local_ids[:, None] == jnp.arange(EXP_GROUP, dtype=jnp.int32)[None, :]).astype(
        jnp.int32
    )
    slot_rank = jnp.sum((jnp.cumsum(onehot, axis=0) - 1) * onehot, axis=1)
    owned = (local_ids >= 0) & (local_ids < EXP_GROUP)
    target = jnp.where(owned, local_ids * CAP + slot_rank, bucket_total)
    pair_index = jnp.arange(pair_total, dtype=jnp.int32)
    slot_token = (
        jnp.full((bucket_total + 1,), block_rows, jnp.int32)
        .at[target]
        .set(pair_index // top_k)[:bucket_total]
    )
    slot_pair = (
        jnp.full((bucket_total + 1,), pair_total, jnp.int32)
        .at[target]
        .set(pair_index)[:bucket_total]
    )
    padded_in = jnp.concatenate([all_in[0], jnp.zeros((1, width), BF16)], axis=0)
    padded_grad = jnp.concatenate([all_grad[0], jnp.zeros((1, width), BF16)], axis=0)
    padded_gates = jnp.concatenate([all_gates.reshape(pair_total), jnp.zeros((1,), BF16)], axis=0)
    holder_expert = lax.dynamic_slice_in_dim(shard_of, group_now, 1, 0)[0] // shards
    send_token = slot_token.reshape(EXP_GROUP, CAP)[holder_expert]
    send_pair = slot_pair.reshape(EXP_GROUP, CAP)[holder_expert]
    rows_in = exchange(padded_in[send_token]).reshape(positions * CAP, width)
    rows_grad = exchange(padded_grad[send_token]).reshape(positions * CAP, width)
    row_gates = exchange(padded_gates[send_pair]).reshape(positions * CAP).astype(F32)
    input_part, gate_part, gate_grad, up_grad, gate_weighted = expert_backward(
        rows_in, rows_grad, row_gates, w_gate[0, 0], w_up[0, 0], w_down[0, 0]
    )
    grad_gate, grad_up, grad_down = weight_grads(
        rows_in, rows_grad, gate_grad, up_grad, gate_weighted
    )
    back_in = exchange(input_part.reshape(positions, CAP, width))
    back_gates = exchange(gate_part.reshape(positions, CAP))
    token_of_row = send_token.reshape(positions * CAP)
    pair_of_row = send_pair.reshape(positions * CAP)
    back_rows = back_in.reshape(positions * CAP, width).astype(F32)
    back_terms = back_gates.reshape(positions * CAP).astype(F32)
    block_input = (
        jnp.zeros((block_rows + 1, width), F32).at[token_of_row].add(back_rows)[:block_rows]
    )
    block_gates = jnp.zeros((pair_total + 1,), F32).at[pair_of_row].add(back_terms)[:pair_total]
    scatter = functools.partial(
        lax.psum_scatter, axis_name="group", scatter_dimension=1, tiled=True
    )
    mine_input = scatter(block_input[None])
    mine_gates = scatter(block_gates.reshape(1, block_rows, top_k))
    return (
        mine_input.astype(BF16),
        mine_gates,
        grad_gate[None, None],
        grad_up[None, None],
        grad_down[None, None],
    )


def build_message(tok_ref, grad_ref, gates_ref, routes_ref, out_ref):
    width = tok_ref.shape[1]
    out_ref[:, :width] = tok_ref[...]
    out_ref[:, width : 2 * width] = grad_ref[...]
    rows, top_k = routes_ref.shape
    lane = lax.broadcasted_iota(jnp.int32, (rows, LANES), 1)
    routes = routes_ref[...]
    gates = gates_ref[...].astype(F32)
    dense = jnp.zeros((rows, LANES), F32)
    for k in range(top_k):
        chosen = routes[:, k : k + 1]
        dense = jnp.where(lane == chosen, gates[:, k : k + 1], dense)
        dense = jnp.where(lane == chosen + LANES // 2, 1.0, dense)
    out_ref[:, 2 * width :] = dense.astype(BF16)


def dot_tt(a, b, da, db):
    return lax.dot_general(a, b, (((da,), (db,)), ((), ())), preferred_element_type=F32)


def expert_kernel(
    which_ref, near_ref, far_ref, wg_ref, wu_ref, wd_ref,
    ret_near_ref, ret_far_ref, rin_ref, rgrad_ref, gg_ref, ug_ref, gw_ref,
):
    which = which_ref[0]
    half, full = near_ref.shape
    width = rin_ref.shape[1]
    slots = rin_ref.shape[0]
    total = 2 * half
    lane = lax.broadcasted_iota(jnp.int32, (8, LANES), 1)
    pick_gate = jnp.where(lane == which, 1.0, 0.0).astype(BF16)
    pick_mask = jnp.where(lane == which + LANES // 2, 1.0, 0.0).astype(BF16)
    extra = jnp.concatenate([near_ref[:, 2 * width :], far_ref[:, 2 * width :]], axis=0)
    gate_row = dot_tt(pick_gate, extra, 1, 1)
    mask_row = dot_tt(pick_mask, extra, 1, 1)
    before = (
        lax.broadcasted_iota(jnp.int32, (total, total), 0)
        < lax.broadcasted_iota(jnp.int32, (total, total), 1)
    )
    before = jnp.where(before, 1.0, 0.0).astype(BF16)
    rank_row = dot_tt(mask_row.astype(BF16), before, 1, 0)
    slot = lax.broadcasted_iota(jnp.int32, (slots, total), 0)
    hit = (slot == rank_row[:1].astype(jnp.int32)) & (mask_row[:1] > 0.5)
    select_f = jnp.where(hit, 1.0, 0.0)
    select = select_f.astype(BF16)
    row_gates = jnp.sum(select_f * gate_row[:1], axis=1, keepdims=True)
    s_near, s_far = select[:, :half], select[:, half:]

    def rows_of(lo):
        cols = slice(lo, lo + width)
        return (
            dot_tt(s_near, near_ref[:, cols], 1, 0) + dot_tt(s_far, far_ref[:, cols], 1, 0)
        ).astype(BF16)

    rows_in = rows_of(0)
    rin_ref[...] = rows_in
    rows_grad = rows_of(width)
    rgrad_ref[...] = rows_grad
    gate_pre = dot_tt(rows_in, wg_ref[...], 1, 1)
    up_pre = dot_tt(rows_in, wu_ref[...], 1, 1)
    back = dot_tt(rows_grad, wd_ref[...], 1, 1)
    sigmoid = jax.nn.sigmoid(gate_pre)
    swish_gate = gate_pre * sigmoid
    hidden = swish_gate * up_pre
    gate_part = jnp.sum(back * hidden, axis=1, keepdims=True)
    hidden_grad = row_gates * back
    gate_grad = (hidden_grad * up_pre * sigmoid * (1.0 + gate_pre * (1.0 - sigmoid))).astype(BF16)
    up_grad = (hidden_grad * swish_gate).astype(BF16)
    gg_ref[...] = gate_grad
    ug_ref[...] = up_grad
    gw_ref[...] = (row_gates * hidden).astype(BF16)
    input_part = (
        dot_tt(gate_grad, wg_ref[...], 1, 0) + dot_tt(up_grad, wu_ref[...], 1, 0)
    ).astype(BF16)
    gate_lane = lax.broadcasted_iota(jnp.int32, (slots, LANES), 1)
    gate_cols = jnp.where(gate_lane == which, gate_part, 0.0).astype(BF16)
    for s, ref in ((s_near, ret_near_ref), (s_far, ret_far_ref)):
        ref[:, :width] = dot_tt(s, input_part, 0, 0).astype(BF16)
        ref[:, width:] = dot_tt(s, gate_cols, 0, 0).astype(BF16)


def weight_kernel(a_ref, b_ref, out_ref):
    out_ref[...] = dot_tt(a_ref[...], b_ref[...], 0, 0).astype(BF16)


def weight_grad(a, b, tile):
    rows, hidden = a.shape
    width = b.shape[1]
    return pl.pallas_call(
        weight_kernel,
        grid=(hidden // tile,),
        in_specs=[
            pl.BlockSpec((rows, tile), lambda i: (0, i)),
            pl.BlockSpec((rows, width), lambda i: (0, 0)),
        ],
        out_specs=pl.BlockSpec((tile, width), lambda i: (i, 0)),
        out_shape=jax.ShapeDtypeStruct((hidden, width), BF16),
        name="weight_grad",
    )(a, b)


def final_kernel(a_ref, b_ref, c_ref, d_ref, routes_ref, in_ref, gate_ref):
    total = (
        a_ref[...].astype(F32) + b_ref[...].astype(F32) + c_ref[...].astype(F32)
        + d_ref[...].astype(F32)
    )
    width = in_ref.shape[1]
    in_ref[...] = total[:, :width].astype(BF16)
    dense = total[:, width:]
    rows, top_k = routes_ref.shape
    routes = routes_ref[...]
    lane = lax.broadcasted_iota(jnp.int32, dense.shape, 1)
    place = lax.broadcasted_iota(jnp.int32, (rows, top_k), 1)
    out = jnp.zeros((rows, top_k), F32)
    for k in range(top_k):
        value = jnp.sum(jnp.where(lane == routes[:, k : k + 1], dense, 0.0), axis=1, keepdims=True)
        out = jnp.where(place == k, value, out)
    gate_ref[...] = out


def whole(memory=pltpu.VMEM):
    return pl.BlockSpec(memory_space=memory)


def swap(x, axes, bits):
    sizes = 1
    for a in axes:
        sizes *= lax.axis_size(a)
    return lax.ppermute(x, axes, [(i, i ^ bits) for i in range(sizes)])


def spread(x, axes):
    count = 1
    for a in axes:
        count *= lax.axis_size(a)
    return [x] + [swap(x, axes, k) for k in range(1, count)]


def block_local(tokens, out_grad, gates, routes, shard_of, w_gate, w_up, w_down):
    group_now = lax.axis_index("x")
    width = tokens.shape[2]
    rows = tokens.shape[1]
    hidden = w_gate.shape[2]
    top_k = routes.shape[2]
    full = 2 * width + LANES
    back_width = width + LANES
    message = pl.pallas_call(
        build_message,
        in_specs=[whole()] * 4,
        out_specs=whole(),
        out_shape=jax.ShapeDtypeStruct((rows, full), BF16),
        name="build_message",
    )(tokens[0], out_grad[0], gates[0], routes[0])
    line = jnp.concatenate(spread(message, ("z",)), axis=0)
    near = jnp.concatenate(spread(line, ("x", "y")), axis=0)
    far = swap(near, ("core",), 1)
    place = (lax.axis_index("z") * 2 + lax.axis_index("y")) * 2 + lax.axis_index("core")
    which = (shard_of[group_now, place] + group_now * EXP_GROUP).astype(jnp.int32).reshape(1)
    half = near.shape[0]
    slots = lax.axis_size("z") * lax.axis_size("y") * lax.axis_size("core") * CAP
    ret_near, ret_far, rows_in, rows_grad, gate_grad, up_grad, weighted = pl.pallas_call(
        expert_kernel,
        in_specs=[whole(pltpu.SMEM)] + [whole()] * 5,
        out_specs=[whole()] * 7,
        out_shape=[
            jax.ShapeDtypeStruct((half, back_width), BF16),
            jax.ShapeDtypeStruct((half, back_width), BF16),
            jax.ShapeDtypeStruct((slots, width), BF16),
            jax.ShapeDtypeStruct((slots, width), BF16),
            jax.ShapeDtypeStruct((slots, hidden), BF16),
            jax.ShapeDtypeStruct((slots, hidden), BF16),
            jax.ShapeDtypeStruct((slots, hidden), BF16),
        ],
        compiler_params=pltpu.CompilerParams(vmem_limit_bytes=VMEM_LIMIT),
        name="expert",
    )(which, near, far, w_gate[0, 0], w_up[0, 0], w_down[0, 0])
    grad_gate = weight_grad(gate_grad, rows_in, 256)
    grad_up = weight_grad(up_grad, rows_in, 256)
    grad_down = weight_grad(weighted, rows_grad, 256)
    peer = swap(ret_far, ("core",), 1)
    summed = (ret_near.astype(F32) + peer.astype(F32)).astype(BF16)
    quarter = half // 4
    pieces = [summed[k * quarter : (k + 1) * quarter] for k in range(4)]
    got = [pieces[0]] + [swap(pieces[k], ("x", "y"), k) for k in range(1, 4)]
    summed = sum(g.astype(F32) for g in got).astype(BF16)
    pieces = [summed[k * rows : (k + 1) * rows] for k in range(4)]
    got = [pieces[0]] + [swap(pieces[k], ("z",), k) for k in range(1, 4)]
    mine_input, mine_gates = pl.pallas_call(
        final_kernel,
        in_specs=[whole()] * 5,
        out_specs=[whole()] * 2,
        out_shape=[
            jax.ShapeDtypeStruct((rows, width), BF16),
            jax.ShapeDtypeStruct((rows, top_k), F32),
        ],
        name="finish",
    )(*got, routes[0])
    return (
        mine_input[None],
        mine_gates[None],
        grad_gate[None, None],
        grad_up[None, None],
        grad_down[None, None],
    )


def mapped(local, mesh, group, expert):
    return jax.shard_map(
        local,
        mesh=mesh,
        in_specs=(
            P(expert, group, None),
            P(expert, group, None),
            P(expert, group, None),
            P(expert, group, None),
            P(),
            P(group, expert, None, None),
            P(group, expert, None, None),
            P(group, expert, None, None),
        ),
        out_specs=(
            P(expert, group, None),
            P(expert, group, None),
            P(group, expert, None, None),
            P(group, expert, None, None),
            P(group, expert, None, None),
        ),
        check_vma=False,
    )


def solution(mesh):
    if mesh.shape["group"] == 2 and mesh.shape["expert"] == 16:
        split = Mesh(mesh.devices.reshape(2, 4, 2, 2), ("x", "z", "y", "core"))
        return mapped(block_local, split, "x", ("z", "y", "core"))
    return mapped(general_local, mesh, "group", "expert")
```

```python
import functools

import jax
import jax.numpy as jnp
from jax import lax
from jax.experimental import pallas as pl
from jax.experimental.pallas import tpu as pltpu
from jax.sharding import Mesh
from jax.sharding import PartitionSpec as P

EXP_GROUP = 16
CAP = 8
LANES = 128
F32 = jnp.float32
BF16 = jnp.bfloat16


def expert_backward(rows_in, rows_grad, row_gates, gate_shard, up_shard, down_shard):
    contraction_dims = (((1,), (1,)), ((), ()))
    gate_pre = lax.dot_general(rows_in, gate_shard, contraction_dims, preferred_element_type=F32)
    up_pre = lax.dot_general(rows_in, up_shard, contraction_dims, preferred_element_type=F32)
    back_hidden = lax.dot_general(
        rows_grad, down_shard, contraction_dims, preferred_element_type=F32
    )
    sigmoid = jax.nn.sigmoid(gate_pre)
    swish_gate = gate_pre * sigmoid
    hidden = swish_gate * up_pre
    gate_part = jnp.sum(back_hidden * hidden, axis=1).astype(BF16)
    hidden_grad = row_gates[:, None] * back_hidden
    gate_grad = (hidden_grad * up_pre * sigmoid * (1.0 + gate_pre * (1.0 - sigmoid))).astype(BF16)
    up_grad = (hidden_grad * swish_gate).astype(BF16)
    input_part = (
        jnp.dot(gate_grad, gate_shard, preferred_element_type=F32)
        + jnp.dot(up_grad, up_shard, preferred_element_type=F32)
    ).astype(BF16)
    gate_weighted = (row_gates[:, None] * hidden).astype(BF16)
    return (input_part, gate_part, gate_grad, up_grad, gate_weighted)


def weight_grads(rows_in, rows_grad, gate_grad, up_grad, gate_weighted):
    contraction_dims = (((0,), (0,)), ((), ()))

    def one(a, b):
        return lax.dot_general(a, b, contraction_dims, preferred_element_type=F32).astype(BF16)

    return one(gate_grad, rows_in), one(up_grad, rows_in), one(gate_weighted, rows_grad)


def exchange(x):
    return lax.all_to_all(x, "expert", split_axis=0, concat_axis=0, tiled=True)


def general_local(tokens, out_grad, gates, routes, shard_of, w_gate, w_up, w_down):
    positions = lax.axis_size("expert")
    group_now = lax.axis_index("group")
    shards = positions // EXP_GROUP
    gather = functools.partial(lax.all_gather, axis_name="group", axis=1, tiled=True)
    all_in, all_grad, all_gates, all_ids = (
        gather(tokens),
        gather(out_grad),
        gather(gates),
        gather(routes),
    )
    width = tokens.shape[2]
    block_rows = all_in.shape[1]
    top_k = routes.shape[2]
    pair_total = block_rows * top_k
    bucket_total = EXP_GROUP * CAP
    local_ids = all_ids.reshape(pair_total) - group_now * EXP_GROUP
    onehot = (local_ids[:, None] == jnp.arange(EXP_GROUP, dtype=jnp.int32)[None, :]).astype(
        jnp.int32
    )
    slot_rank = jnp.sum((jnp.cumsum(onehot, axis=0) - 1) * onehot, axis=1)
    owned = (local_ids >= 0) & (local_ids < EXP_GROUP)
    target = jnp.where(owned, local_ids * CAP + slot_rank, bucket_total)
    pair_index = jnp.arange(pair_total, dtype=jnp.int32)
    slot_token = (
        jnp.full((bucket_total + 1,), block_rows, jnp.int32)
        .at[target]
        .set(pair_index // top_k)[:bucket_total]
    )
    slot_pair = (
        jnp.full((bucket_total + 1,), pair_total, jnp.int32)
        .at[target]
        .set(pair_index)[:bucket_total]
    )
    padded_in = jnp.concatenate([all_in[0], jnp.zeros((1, width), BF16)], axis=0)
    padded_grad = jnp.concatenate([all_grad[0], jnp.zeros((1, width), BF16)], axis=0)
    padded_gates = jnp.concatenate([all_gates.reshape(pair_total), jnp.zeros((1,), BF16)], axis=0)
    holder_expert = lax.dynamic_slice_in_dim(shard_of, group_now, 1, 0)[0] // shards
    send_token = slot_token.reshape(EXP_GROUP, CAP)[holder_expert]
    send_pair = slot_pair.reshape(EXP_GROUP, CAP)[holder_expert]
    rows_in = exchange(padded_in[send_token]).reshape(positions * CAP, width)
    rows_grad = exchange(padded_grad[send_token]).reshape(positions * CAP, width)
    row_gates = exchange(padded_gates[send_pair]).reshape(positions * CAP).astype(F32)
    input_part, gate_part, gate_grad, up_grad, gate_weighted = expert_backward(
        rows_in, rows_grad, row_gates, w_gate[0, 0], w_up[0, 0], w_down[0, 0]
    )
    grad_gate, grad_up, grad_down = weight_grads(
        rows_in, rows_grad, gate_grad, up_grad, gate_weighted
    )
    back_in = exchange(input_part.reshape(positions, CAP, width))
    back_gates = exchange(gate_part.reshape(positions, CAP))
    token_of_row = send_token.reshape(positions * CAP)
    pair_of_row = send_pair.reshape(positions * CAP)
    back_rows = back_in.reshape(positions * CAP, width).astype(F32)
    back_terms = back_gates.reshape(positions * CAP).astype(F32)
    block_input = (
        jnp.zeros((block_rows + 1, width), F32).at[token_of_row].add(back_rows)[:block_rows]
    )
    block_gates = jnp.zeros((pair_total + 1,), F32).at[pair_of_row].add(back_terms)[:pair_total]
    scatter = functools.partial(
        lax.psum_scatter, axis_name="group", scatter_dimension=1, tiled=True
    )
    mine_input = scatter(block_input[None])
    mine_gates = scatter(block_gates.reshape(1, block_rows, top_k))
    return (
        mine_input.astype(BF16),
        mine_gates,
        grad_gate[None, None],
        grad_up[None, None],
        grad_down[None, None],
    )


def dot_on(a, b, da, db):
    return lax.dot_general(a, b, (((da,), (db,)), ((), ())), preferred_element_type=F32)


def build_message(tok_ref, grad_ref, gates_ref, routes_ref, out_ref):
    width = tok_ref.shape[1]
    out_ref[:, :width] = tok_ref[...]
    out_ref[:, width + LANES :] = grad_ref[...]
    rows, top_k = routes_ref.shape
    lane = lax.broadcasted_iota(jnp.int32, (rows, LANES), 1)
    routes = routes_ref[...]
    gates = gates_ref[...].astype(F32)
    dense = jnp.zeros((rows, LANES), F32)
    for k in range(top_k):
        chosen = routes[:, k : k + 1]
        dense = jnp.where(lane == chosen, gates[:, k : k + 1], dense)
        dense = jnp.where(lane == chosen + LANES // 2, 1.0, dense)
    out_ref[:, width : width + LANES] = dense.astype(BF16)


def my_expert(shard_ref):
    group = lax.axis_index("x")
    place = (lax.axis_index("z") * 2 + lax.axis_index("y")) * 2 + lax.axis_index("core")
    return shard_ref[group, place] + group * EXP_GROUP


def load(src_ref, dst_ref, sems, parts=4):
    step = src_ref.shape[0] // parts
    copies = []
    for i in range(parts):
        part = slice(i * step, (i + 1) * step)
        copies.append(pltpu.make_async_copy(src_ref.at[part], dst_ref.at[part], sems.at[i]))
        copies[-1].start()
    return copies


def forward_kernel(
    shard_ref, near_ref, far_ref, wg_hbm, wu_hbm, wd_hbm,
    rin_ref, hidden_ref, gfac_ref, ufac_ref, gw_ref, snear_ref, sfar_ref, wg_ref, wu_ref, wd_ref,
    sems,
):
    loads = [
        load(src, dst, sems.at[n])
        for n, (src, dst) in enumerate(((wg_hbm, wg_ref), (wu_hbm, wu_ref), (wd_hbm, wd_ref)))
    ]
    which = my_expert(shard_ref)
    core = lax.axis_index("core")
    half = near_ref.shape[0]
    slots, width = rin_ref.shape
    total = 2 * half
    lane = lax.broadcasted_iota(jnp.int32, (8, LANES), 1)
    pick_gate = jnp.where(lane == which, 1.0, 0.0).astype(BF16)
    pick_mask = jnp.where(lane == which + LANES // 2, 1.0, 0.0).astype(BF16)
    extra = jnp.concatenate([near_ref[:, width:], far_ref[:, width:]], axis=0)
    gate_row = dot_on(pick_gate, extra, 1, 1)
    mask_row = dot_on(pick_mask, extra, 1, 1)
    before = (
        lax.broadcasted_iota(jnp.int32, (total, total), 0)
        < lax.broadcasted_iota(jnp.int32, (total, total), 1)
    )
    before = jnp.where(before, 1.0, 0.0).astype(BF16)
    rank_row = dot_on(mask_row.astype(BF16), before, 1, 0)
    slot = lax.broadcasted_iota(jnp.int32, (slots, total), 0)
    hit = (slot == rank_row[:1].astype(jnp.int32)) & (mask_row[:1] > 0.5)
    select_f = jnp.where(hit, 1.0, 0.0)
    select = select_f.astype(BF16)
    row_gates = jnp.sum(select_f * gate_row[:1], axis=1, keepdims=True)
    s_near, s_far = select[:, :half], select[:, half:]
    rows_in = (
        dot_on(s_near, near_ref[:, :width], 1, 0) + dot_on(s_far, far_ref[:, :width], 1, 0)
    ).astype(BF16)
    rin_ref[...] = rows_in
    row = lax.broadcasted_iota(jnp.int32, (half, half), 0)
    col = lax.broadcasted_iota(jnp.int32, (half, half), 1)
    turned = (col % 8) + 8 * ((col // 32) + 4 * ((col // 8) % 4))
    turn = jnp.where(row == turned, 1.0, 0.0).astype(BF16)
    for part, ref, turn_it in ((s_near, snear_ref, core > 0), (s_far, sfar_ref, core == 0)):
        ref[...] = jnp.where(turn_it & (MIXED != MIXED_T), dot_on(part, turn, 1, 0), part.astype(F32)).astype(BF16)
    for copy in loads[0]:
        copy.wait()
    gate_pre = dot_on(rows_in, wg_ref[...], 1, 1)
    for copy in loads[1]:
        copy.wait()
    up_pre = dot_on(rows_in, wu_ref[...], 1, 1)
    sigmoid = jax.nn.sigmoid(gate_pre)
    swish_gate = gate_pre * sigmoid
    hidden = swish_gate * up_pre
    hidden_ref[...] = hidden
    gw_ref[...] = (row_gates * hidden).astype(BF16)
    ufac_ref[...] = row_gates * swish_gate
    gfac_ref[...] = row_gates * (up_pre * sigmoid * (1.0 + gate_pre * (1.0 - sigmoid)))
    for copy in loads[2]:
        copy.wait()


def backward_kernel(
    shard_ref, near_ref, far_ref, snear_ref, sfar_ref, hidden_ref, gfac_ref, ufac_ref,
    wg_ref, wu_ref, wd_ref,
    ret_near_ref, ret_far_ref, rgrad_ref, gg_ref, ug_ref,
):
    which = my_expert(shard_ref)
    slots, width = rgrad_ref.shape
    s_near, s_far = snear_ref[...], sfar_ref[...]
    rows_grad = (dot_on(s_near, near_ref[...], 1, 0) + dot_on(s_far, far_ref[...], 1, 0)).astype(
        BF16
    )
    rgrad_ref[...] = rows_grad
    back = dot_on(rows_grad, wd_ref[...], 1, 1)
    gate_grad = (back * gfac_ref[...]).astype(BF16)
    up_grad = (back * ufac_ref[...]).astype(BF16)
    gg_ref[...] = gate_grad
    ug_ref[...] = up_grad
    gate_part = jnp.sum(back * hidden_ref[...], axis=1, keepdims=True)
    input_part = (
        dot_on(gate_grad, wg_ref[...], 1, 0) + dot_on(up_grad, wu_ref[...], 1, 0)
    ).astype(BF16)
    gate_lane = lax.broadcasted_iota(jnp.int32, (slots, LANES), 1)
    gate_cols = jnp.where(gate_lane == which, gate_part, 0.0).astype(BF16)
    for s, ref in ((s_near, ret_near_ref), (s_far, ret_far_ref)):
        ref[:, :width] = dot_on(s, input_part, 0, 0).astype(BF16)
        ref[:, width:] = dot_on(s, gate_cols, 0, 0).astype(BF16)


def weight_kernel(tile, count, *refs):
    pairs = [(refs[2 * n], refs[2 * n + 1]) for n in range(count)]
    outs = refs[2 * count : 3 * count]
    held, sems = refs[3 * count :]
    steps = outs[0].shape[0] // tile
    copies = []
    for n, ((a_ref, b_ref), out) in enumerate(zip(pairs, outs)):
        for i in range(steps):
            part = slice(i * tile, (i + 1) * tile)
            held[n, part, :] = dot_on(a_ref[:, part], b_ref[...], 0, 0).astype(BF16)
            copy = pltpu.make_async_copy(held.at[n, part, :], out.at[part, :], sems.at[n, i])
            copy.start()
            copies.append(copy)
    for copy in copies:
        copy.wait()


def weight_grads_of(*pairs, tile=256):
    count = len(pairs)
    hidden = pairs[0][0].shape[1]
    width = pairs[0][1].shape[1]
    flat = [in_vmem(v) for pair in pairs for v in pair]
    return pl.pallas_call(
        functools.partial(weight_kernel, tile, count),
        in_specs=[whole()] * len(flat),
        out_specs=[whole(pl.ANY)] * count,
        out_shape=[jax.ShapeDtypeStruct((hidden, width), BF16)] * count,
        scratch_shapes=[
            pltpu.VMEM((count, hidden, width), BF16),
            pltpu.SemaphoreType.DMA((count, hidden // tile)),
        ],
        compiler_params=pltpu.CompilerParams(vmem_limit_bytes=20 * 1024 * 1024),
        name="weight_grads",
    )(*flat)


def sum_kernel(a_ref, b_ref, c_ref, d_ref, out_ref):
    out_ref[...] = (
        a_ref[...].astype(F32) + b_ref[...].astype(F32) + c_ref[...].astype(F32)
        + d_ref[...].astype(F32)
    ).astype(BF16)


def final_kernel(a_ref, b_ref, c_ref, d_ref, routes_ref, in_ref, gate_ref):
    total = (
        a_ref[...].astype(F32) + b_ref[...].astype(F32) + c_ref[...].astype(F32)
        + d_ref[...].astype(F32)
    )
    width = in_ref.shape[1]
    in_ref[...] = total[:, :width].astype(BF16)
    dense = total[:, width:]
    rows, top_k = routes_ref.shape
    routes = routes_ref[...]
    lane = lax.broadcasted_iota(jnp.int32, dense.shape, 1)
    place = lax.broadcasted_iota(jnp.int32, (rows, top_k), 1)
    out = jnp.zeros((rows, top_k), F32)
    for k in range(top_k):
        value = jnp.sum(jnp.where(lane == routes[:, k : k + 1], dense, 0.0), axis=1, keepdims=True)
        out = jnp.where(place == k, value, out)
    gate_ref[...] = out


MIXED = True
MIXED_T = MIXED
AXES = ("x", "z", "y", "core")


def whole(memory=pltpu.VMEM):
    return pl.BlockSpec(memory_space=memory)


def in_vmem(x):
    return pltpu.with_memory_space_constraint(x, pltpu.VMEM)


def in_hbm(x):
    return pltpu.with_memory_space_constraint(x, pltpu.HBM)


def partner(device, plane, k):
    x, z, y, core = device // 16, device // 4 % 4, device // 2 % 2, device % 2
    if plane:
        x, y = x ^ (k & 1), y ^ (k >> 1)
    else:
        z = z ^ k
    return ((x * 4 + z) * 2 + y) * 2 + core


def swap(value, late, mixed, k):
    pairs = []
    for device in range(32):
        plane = late != (mixed and device % 2 == 1)
        pairs.append((device, partner(device, plane, k)))
    return lax.ppermute(value, AXES, pairs)


def swap_core(value):
    return lax.ppermute(value, AXES, [(d, d ^ 1) for d in range(32)])


def spread(value, late, mixed):
    return [value] + [swap(value, late, mixed, k) for k in (1, 2, 3)]


def join(pieces):
    return jnp.concatenate(pieces, axis=0)


def fold(value, late, mixed):
    part = value.shape[0] // 4
    pieces = [value[k * part : (k + 1) * part] for k in range(4)]
    return [pieces[0]] + [swap(pieces[k], late, mixed, k) for k in (1, 2, 3)]


def block_local(tokens, out_grad, gates, routes, shard_of, w_gate, w_up, w_down):
    width = tokens.shape[2]
    rows = tokens.shape[1]
    hidden = w_gate.shape[2]
    top_k = routes.shape[2]
    back_width = width + LANES
    message = pl.pallas_call(
        build_message,
        in_specs=[whole()] * 4,
        out_specs=whole(),
        out_shape=pltpu.VMEM((rows, back_width + width), BF16),
        name="build_message",
    )(tokens[0], out_grad[0], gates[0], routes[0])
    first = spread(message, False, MIXED)
    t_near = join(spread(join([v[:, :back_width] for v in first]), True, MIXED))
    g_parts = spread(join([v[:, back_width:] for v in first]), True, MIXED)
    t_far = swap_core(t_near)
    half = t_near.shape[0]
    slots = 16 * CAP
    rows_in, act, gate_fac, up_fac, weighted, s_near, s_far, wg, wu, wd = pl.pallas_call(
        forward_kernel,
        in_specs=[whole(pltpu.SMEM)] + [whole()] * 2 + [whole(pltpu.HBM)] * 3,
        out_specs=[whole()] * 10,
        out_shape=[pltpu.VMEM((slots, width), BF16)]
        + [pltpu.VMEM((slots, hidden), F32)] * 3
        + [pltpu.VMEM((slots, hidden), BF16)]
        + [pltpu.VMEM((slots, half), BF16)] * 2
        + [pltpu.VMEM((hidden, width), BF16)] * 3,
        scratch_shapes=[pltpu.SemaphoreType.DMA((3, 4))],
        compiler_params=pltpu.CompilerParams(vmem_limit_bytes=16 * 1024 * 1024),
        name="forward",
    )(shard_of, in_vmem(t_near), in_vmem(t_far), *(in_hbm(w[0, 0]) for w in (w_gate, w_up, w_down)))
    g_parts, s_near = lax.optimization_barrier((g_parts, s_near))
    g_near = join(g_parts)
    g_far = swap_core(g_near)
    ret_near, ret_far, rows_grad, gate_grad, up_grad = pl.pallas_call(
        backward_kernel,
        in_specs=[whole(pltpu.SMEM)] + [whole()] * 10,
        out_specs=[whole()] * 5,
        out_shape=[pltpu.VMEM((half, back_width), BF16)] * 2
        + [pltpu.VMEM((slots, width), BF16)]
        + [pltpu.VMEM((slots, hidden), BF16)] * 2,
        compiler_params=pltpu.CompilerParams(vmem_limit_bytes=16 * 1024 * 1024),
        name="backward",
    )(shard_of, in_vmem(g_near), in_vmem(g_far), s_near, s_far, act, gate_fac, up_fac, wg, wu, wd)
    peer = swap_core(ret_far)
    summed = (ret_near.astype(F32) + peer.astype(F32)).astype(BF16)
    got = fold(summed, True, MIXED)
    grad_gate, grad_up = weight_grads_of((gate_grad, rows_in), (up_grad, rows_in))
    got, grad_gate, grad_up = lax.optimization_barrier((got, grad_gate, grad_up))
    summed = sum(g.astype(F32) for g in got).astype(BF16)
    got = fold(summed, False, MIXED)
    (grad_down,) = weight_grads_of((weighted, rows_grad))
    got, grad_down = lax.optimization_barrier((got, grad_down))
    mine_input, mine_gates = pl.pallas_call(
        final_kernel,
        in_specs=[whole()] * 5,
        out_specs=[whole()] * 2,
        out_shape=[
            jax.ShapeDtypeStruct((rows, width), BF16),
            jax.ShapeDtypeStruct((rows, top_k), F32),
        ],
        name="finish",
    )(*[in_vmem(g) for g in got], routes[0])
    return (
        mine_input[None],
        mine_gates[None],
        grad_gate[None, None],
        grad_up[None, None],
        grad_down[None, None],
    )


def mapped(local, mesh, group, expert):
    return jax.shard_map(
        local,
        mesh=mesh,
        in_specs=(
            P(expert, group, None),
            P(expert, group, None),
            P(expert, group, None),
            P(expert, group, None),
            P(),
            P(group, expert, None, None),
            P(group, expert, None, None),
            P(group, expert, None, None),
        ),
        out_specs=(
            P(expert, group, None),
            P(expert, group, None),
            P(group, expert, None, None),
            P(group, expert, None, None),
            P(group, expert, None, None),
        ),
        check_vma=False,
    )


def solution(mesh):
    if mesh.shape["group"] == 2 and mesh.shape["expert"] == 16:
        split = Mesh(mesh.devices.reshape(2, 4, 2, 2), ("x", "z", "y", "core"))
        return mapped(block_local, split, "x", ("z", "y", "core"))
    return mapped(general_local, mesh, "group", "expert")
```

```python
import functools

import jax
import jax.numpy as jnp
from jax import lax
from jax.experimental import pallas as pl
from jax.experimental.pallas import tpu as pltpu
from jax.sharding import Mesh
from jax.sharding import PartitionSpec as P

EXP_GROUP = 16
CAP = 8
LANES = 128
F32 = jnp.float32
BF16 = jnp.bfloat16


def expert_backward(rows_in, rows_grad, row_gates, gate_shard, up_shard, down_shard):
    contraction_dims = (((1,), (1,)), ((), ()))
    gate_pre = lax.dot_general(rows_in, gate_shard, contraction_dims, preferred_element_type=F32)
    up_pre = lax.dot_general(rows_in, up_shard, contraction_dims, preferred_element_type=F32)
    back_hidden = lax.dot_general(
        rows_grad, down_shard, contraction_dims, preferred_element_type=F32
    )
    sigmoid = jax.nn.sigmoid(gate_pre)
    swish_gate = gate_pre * sigmoid
    hidden = swish_gate * up_pre
    gate_part = jnp.sum(back_hidden * hidden, axis=1).astype(BF16)
    hidden_grad = row_gates[:, None] * back_hidden
    gate_grad = (hidden_grad * up_pre * sigmoid * (1.0 + gate_pre * (1.0 - sigmoid))).astype(BF16)
    up_grad = (hidden_grad * swish_gate).astype(BF16)
    input_part = (
        jnp.dot(gate_grad, gate_shard, preferred_element_type=F32)
        + jnp.dot(up_grad, up_shard, preferred_element_type=F32)
    ).astype(BF16)
    gate_weighted = (row_gates[:, None] * hidden).astype(BF16)
    return (input_part, gate_part, gate_grad, up_grad, gate_weighted)


def weight_grads(rows_in, rows_grad, gate_grad, up_grad, gate_weighted):
    contraction_dims = (((0,), (0,)), ((), ()))

    def one(a, b):
        return lax.dot_general(a, b, contraction_dims, preferred_element_type=F32).astype(BF16)

    return one(gate_grad, rows_in), one(up_grad, rows_in), one(gate_weighted, rows_grad)


def exchange(x):
    return lax.all_to_all(x, "expert", split_axis=0, concat_axis=0, tiled=True)


def general_local(tokens, out_grad, gates, routes, shard_of, w_gate, w_up, w_down):
    positions = lax.axis_size("expert")
    group_now = lax.axis_index("group")
    shards = positions // EXP_GROUP
    gather = functools.partial(lax.all_gather, axis_name="group", axis=1, tiled=True)
    all_in, all_grad, all_gates, all_ids = (
        gather(tokens),
        gather(out_grad),
        gather(gates),
        gather(routes),
    )
    width = tokens.shape[2]
    block_rows = all_in.shape[1]
    top_k = routes.shape[2]
    pair_total = block_rows * top_k
    bucket_total = EXP_GROUP * CAP
    local_ids = all_ids.reshape(pair_total) - group_now * EXP_GROUP
    onehot = (local_ids[:, None] == jnp.arange(EXP_GROUP, dtype=jnp.int32)[None, :]).astype(
        jnp.int32
    )
    slot_rank = jnp.sum((jnp.cumsum(onehot, axis=0) - 1) * onehot, axis=1)
    owned = (local_ids >= 0) & (local_ids < EXP_GROUP)
    target = jnp.where(owned, local_ids * CAP + slot_rank, bucket_total)
    pair_index = jnp.arange(pair_total, dtype=jnp.int32)
    slot_token = (
        jnp.full((bucket_total + 1,), block_rows, jnp.int32)
        .at[target]
        .set(pair_index // top_k)[:bucket_total]
    )
    slot_pair = (
        jnp.full((bucket_total + 1,), pair_total, jnp.int32)
        .at[target]
        .set(pair_index)[:bucket_total]
    )
    padded_in = jnp.concatenate([all_in[0], jnp.zeros((1, width), BF16)], axis=0)
    padded_grad = jnp.concatenate([all_grad[0], jnp.zeros((1, width), BF16)], axis=0)
    padded_gates = jnp.concatenate([all_gates.reshape(pair_total), jnp.zeros((1,), BF16)], axis=0)
    holder_expert = lax.dynamic_slice_in_dim(shard_of, group_now, 1, 0)[0] // shards
    send_token = slot_token.reshape(EXP_GROUP, CAP)[holder_expert]
    send_pair = slot_pair.reshape(EXP_GROUP, CAP)[holder_expert]
    rows_in = exchange(padded_in[send_token]).reshape(positions * CAP, width)
    rows_grad = exchange(padded_grad[send_token]).reshape(positions * CAP, width)
    row_gates = exchange(padded_gates[send_pair]).reshape(positions * CAP).astype(F32)
    input_part, gate_part, gate_grad, up_grad, gate_weighted = expert_backward(
        rows_in, rows_grad, row_gates, w_gate[0, 0], w_up[0, 0], w_down[0, 0]
    )
    grad_gate, grad_up, grad_down = weight_grads(
        rows_in, rows_grad, gate_grad, up_grad, gate_weighted
    )
    back_in = exchange(input_part.reshape(positions, CAP, width))
    back_gates = exchange(gate_part.reshape(positions, CAP))
    token_of_row = send_token.reshape(positions * CAP)
    pair_of_row = send_pair.reshape(positions * CAP)
    back_rows = back_in.reshape(positions * CAP, width).astype(F32)
    back_terms = back_gates.reshape(positions * CAP).astype(F32)
    block_input = (
        jnp.zeros((block_rows + 1, width), F32).at[token_of_row].add(back_rows)[:block_rows]
    )
    block_gates = jnp.zeros((pair_total + 1,), F32).at[pair_of_row].add(back_terms)[:pair_total]
    scatter = functools.partial(
        lax.psum_scatter, axis_name="group", scatter_dimension=1, tiled=True
    )
    mine_input = scatter(block_input[None])
    mine_gates = scatter(block_gates.reshape(1, block_rows, top_k))
    return (
        mine_input.astype(BF16),
        mine_gates,
        grad_gate[None, None],
        grad_up[None, None],
        grad_down[None, None],
    )


def dot_on(a, b, da, db):
    return lax.dot_general(a, b, (((da,), (db,)), ((), ())), preferred_element_type=F32)


def build_message(
    tok_hbm, grad_hbm, gates_hbm, routes_hbm, out_ref, tok_ref, grad_ref, gates_ref, routes_ref, sems
):
    width = tok_ref.shape[1]
    arrivals = (
        (gates_hbm, gates_ref), (routes_hbm, routes_ref), (tok_hbm, tok_ref), (grad_hbm, grad_ref),
    )
    copies = [pltpu.make_async_copy(*pair, sems.at[n]) for n, pair in enumerate(arrivals)]
    for copy in copies:
        copy.start()
    for copy in copies:
        copy.wait()
    out_ref[:, :width] = tok_ref[...]
    out_ref[:, width + LANES :] = grad_ref[...]
    rows, top_k = routes_ref.shape
    lane = lax.broadcasted_iota(jnp.int32, (rows, LANES), 1)
    routes = routes_ref[...]
    gates = gates_ref[...].astype(F32)
    dense = jnp.zeros((rows, LANES), F32)
    for k in range(top_k):
        chosen = routes[:, k : k + 1]
        dense = jnp.where(lane == chosen, gates[:, k : k + 1], dense)
        dense = jnp.where(lane == chosen + LANES // 2, 1.0, dense)
    out_ref[:, width : width + LANES] = dense.astype(BF16)


def my_expert(shard_ref):
    group = lax.axis_index("x")
    place = (lax.axis_index("z") * 2 + lax.axis_index("y")) * 2 + lax.axis_index("core")
    return shard_ref[group, place] + group * EXP_GROUP


def load(src_ref, dst_ref, sems, parts=4):
    step = src_ref.shape[0] // parts
    copies = []
    for i in range(parts):
        part = slice(i * step, (i + 1) * step)
        copies.append(pltpu.make_async_copy(src_ref.at[part], dst_ref.at[part], sems.at[i]))
        copies[-1].start()
    return copies


def prefetch_kernel(*refs):
    count = (len(refs) - 1) // 2
    sems = refs[-1]
    copies = []
    for n in range(count):
        copies += load(refs[n], refs[count + n], sems.at[n])
    for copy in copies:
        copy.wait()


def prefetch(*weights):
    return pl.pallas_call(
        prefetch_kernel,
        in_specs=[whole(pltpu.HBM)] * len(weights),
        out_specs=[whole()] * len(weights),
        out_shape=[pltpu.VMEM(w.shape, w.dtype) for w in weights],
        scratch_shapes=[pltpu.SemaphoreType.DMA((len(weights), 4))],
        compiler_params=limit(2),
        name="prefetch",
    )(*(in_hbm(w) for w in weights))


def forward_kernel(
    shard_ref, near_ref, far_ref, wg_ref, wu_ref,
    rin_ref, hidden_ref, gfac_ref, ufac_ref, gw_ref, snear_ref, sfar_ref,
):
    which = my_expert(shard_ref)
    core = lax.axis_index("core")
    half = near_ref.shape[0]
    slots, width = rin_ref.shape
    total = 2 * half
    lane = lax.broadcasted_iota(jnp.int32, (8, LANES), 1)
    pick_gate = jnp.where(lane == which, 1.0, 0.0).astype(BF16)
    pick_mask = jnp.where(lane == which + LANES // 2, 1.0, 0.0).astype(BF16)
    extra = jnp.concatenate([near_ref[:, width:], far_ref[:, width:]], axis=0)
    gate_row = dot_on(pick_gate, extra, 1, 1)
    mask_row = dot_on(pick_mask, extra, 1, 1)
    before = (
        lax.broadcasted_iota(jnp.int32, (total, total), 0)
        < lax.broadcasted_iota(jnp.int32, (total, total), 1)
    )
    before = jnp.where(before, 1.0, 0.0).astype(BF16)
    rank_row = dot_on(mask_row.astype(BF16), before, 1, 0)
    slot = lax.broadcasted_iota(jnp.int32, (slots, total), 0)
    hit = (slot == rank_row[:1].astype(jnp.int32)) & (mask_row[:1] > 0.5)
    select_f = jnp.where(hit, 1.0, 0.0)
    select = select_f.astype(BF16)
    row_gates = jnp.sum(select_f * gate_row[:1], axis=1, keepdims=True)
    s_near, s_far = select[:, :half], select[:, half:]
    rows_in = (
        dot_on(s_near, near_ref[:, :width], 1, 0) + dot_on(s_far, far_ref[:, :width], 1, 0)
    ).astype(BF16)
    rin_ref[...] = rows_in
    row = lax.broadcasted_iota(jnp.int32, (half, half), 0)
    col = lax.broadcasted_iota(jnp.int32, (half, half), 1)
    turned = (col % 8) + 8 * ((col // 32) + 4 * ((col // 8) % 4))
    turn = jnp.where(row == turned, 1.0, 0.0).astype(BF16)
    for part, ref, turn_it in ((s_near, snear_ref, core > 0), (s_far, sfar_ref, core == 0)):
        ref[...] = jnp.where(turn_it & (MIXED != MIXED_T), dot_on(part, turn, 1, 0), part.astype(F32)).astype(BF16)
    gate_pre = dot_on(rows_in, wg_ref[...], 1, 1)
    up_pre = dot_on(rows_in, wu_ref[...], 1, 1)
    sigmoid = jax.nn.sigmoid(gate_pre)
    swish_gate = gate_pre * sigmoid
    hidden = swish_gate * up_pre
    hidden_ref[...] = hidden
    gw_ref[...] = (row_gates * hidden).astype(BF16)
    ufac_ref[...] = row_gates * swish_gate
    gfac_ref[...] = row_gates * (up_pre * sigmoid * (1.0 + gate_pre * (1.0 - sigmoid)))


def backward_kernel(
    shard_ref, near_ref, far_ref, snear_ref, sfar_ref, hidden_ref, gfac_ref, ufac_ref,
    wg_ref, wu_ref, wd_ref,
    ret_near_ref, ret_far_ref, rgrad_ref, gg_ref, ug_ref,
):
    which = my_expert(shard_ref)
    slots, width = rgrad_ref.shape
    s_near, s_far = snear_ref[...], sfar_ref[...]
    rows_grad = (dot_on(s_near, near_ref[...], 1, 0) + dot_on(s_far, far_ref[...], 1, 0)).astype(
        BF16
    )
    rgrad_ref[...] = rows_grad
    back = dot_on(rows_grad, wd_ref[...], 1, 1)
    gate_grad = (back * gfac_ref[...]).astype(BF16)
    up_grad = (back * ufac_ref[...]).astype(BF16)
    gg_ref[...] = gate_grad
    ug_ref[...] = up_grad
    gate_part = jnp.sum(back * hidden_ref[...], axis=1, keepdims=True)
    input_part = (
        dot_on(gate_grad, wg_ref[...], 1, 0) + dot_on(up_grad, wu_ref[...], 1, 0)
    ).astype(BF16)
    gate_lane = lax.broadcasted_iota(jnp.int32, (slots, LANES), 1)
    gate_cols = jnp.where(gate_lane == which, gate_part, 0.0).astype(BF16)
    for s, ref in ((s_near, ret_near_ref), (s_far, ret_far_ref)):
        ref[:, :width] = dot_on(s, input_part, 0, 0).astype(BF16)
        ref[:, width:] = dot_on(s, gate_cols, 0, 0).astype(BF16)


def weight_kernel(tile, count, *refs):
    pairs = [(refs[2 * n], refs[2 * n + 1]) for n in range(count)]
    outs = refs[2 * count : 3 * count]
    held, sems = refs[3 * count :]
    steps = outs[0].shape[0] // tile
    copies = []
    for n, ((a_ref, b_ref), out) in enumerate(zip(pairs, outs)):
        for i in range(steps):
            part = slice(i * tile, (i + 1) * tile)
            held[n, part, :] = dot_on(a_ref[:, part], b_ref[...], 0, 0).astype(BF16)
            copy = pltpu.make_async_copy(held.at[n, part, :], out.at[part, :], sems.at[n, i])
            copy.start()
            copies.append(copy)
    for copy in copies:
        copy.wait()


def weight_grads_of(*pairs, tile=256):
    count = len(pairs)
    hidden = pairs[0][0].shape[1]
    width = pairs[0][1].shape[1]
    flat = [in_vmem(v) for pair in pairs for v in pair]
    return pl.pallas_call(
        functools.partial(weight_kernel, tile, count),
        in_specs=[whole()] * len(flat),
        out_specs=[whole(pl.ANY)] * count,
        out_shape=[jax.ShapeDtypeStruct((hidden, width), BF16)] * count,
        scratch_shapes=[
            pltpu.VMEM((count, hidden, width), BF16),
            pltpu.SemaphoreType.DMA((count, hidden // tile)),
        ],
        compiler_params=limit(20),
        name="weight_grads",
    )(*flat)


def sum_kernel(a_ref, b_ref, c_ref, d_ref, out_ref):
    out_ref[...] = (
        a_ref[...].astype(F32) + b_ref[...].astype(F32) + c_ref[...].astype(F32)
        + d_ref[...].astype(F32)
    ).astype(BF16)


def final_kernel(a_ref, b_ref, c_ref, d_ref, routes_ref, in_ref, gate_ref):
    total = (
        a_ref[...].astype(F32) + b_ref[...].astype(F32) + c_ref[...].astype(F32)
        + d_ref[...].astype(F32)
    )
    width = in_ref.shape[1]
    in_ref[...] = total[:, :width].astype(BF16)
    dense = total[:, width:]
    rows, top_k = routes_ref.shape
    routes = routes_ref[...]
    lane = lax.broadcasted_iota(jnp.int32, dense.shape, 1)
    place = lax.broadcasted_iota(jnp.int32, (rows, top_k), 1)
    out = jnp.zeros((rows, top_k), F32)
    for k in range(top_k):
        value = jnp.sum(jnp.where(lane == routes[:, k : k + 1], dense, 0.0), axis=1, keepdims=True)
        out = jnp.where(place == k, value, out)
    gate_ref[...] = out


MIXED = True
MIXED_T = MIXED
AXES = ("x", "z", "y", "core")


def limit(mebibytes):
    return pltpu.CompilerParams(vmem_limit_bytes=mebibytes * 1024 * 1024)


def whole(memory=pltpu.VMEM):
    return pl.BlockSpec(memory_space=memory)


def in_vmem(x):
    return pltpu.with_memory_space_constraint(x, pltpu.VMEM)


def in_hbm(x):
    return pltpu.with_memory_space_constraint(x, pltpu.HBM)


def partner(device, plane, k):
    x, z, y, core = device // 16, device // 4 % 4, device // 2 % 2, device % 2
    if plane:
        x, y = x ^ (k & 1), y ^ (k >> 1)
    else:
        z = z ^ k
    return ((x * 4 + z) * 2 + y) * 2 + core


def swap(value, late, mixed, k):
    pairs = []
    for device in range(32):
        plane = late != (mixed and device % 2 == 1)
        pairs.append((device, partner(device, plane, k)))
    return lax.ppermute(value, AXES, pairs)


def swap_core(value):
    return lax.ppermute(value, AXES, [(d, d ^ 1) for d in range(32)])


def spread(value, late, mixed):
    return [value] + [swap(value, late, mixed, k) for k in (1, 2, 3)]


def join(pieces):
    return jnp.concatenate(pieces, axis=0)


def fold(value, late, mixed):
    part = value.shape[0] // 4
    pieces = [value[k * part : (k + 1) * part] for k in range(4)]
    return [pieces[0]] + [swap(pieces[k], late, mixed, k) for k in (1, 2, 3)]


def block_local(tokens, out_grad, gates, routes, shard_of, w_gate, w_up, w_down):
    width = tokens.shape[2]
    rows = tokens.shape[1]
    hidden = w_gate.shape[2]
    top_k = routes.shape[2]
    back_width = width + LANES
    message = pl.pallas_call(
        build_message,
        in_specs=[whole(pltpu.HBM)] * 4,
        out_specs=whole(),
        scratch_shapes=[
            pltpu.VMEM(v.shape[1:], v.dtype) for v in (tokens, out_grad, gates, routes)
        ]
        + [pltpu.SemaphoreType.DMA((4,))],
        out_shape=pltpu.VMEM((rows, back_width + width), BF16),
        compiler_params=limit(4),
        name="build_message",
    )(*(in_hbm(v[0]) for v in (tokens, out_grad, gates, routes)))
    first = spread(message, False, MIXED)
    wg, wu, wd = prefetch(w_gate[0, 0], w_up[0, 0], w_down[0, 0])
    first, wg, wu, wd = lax.optimization_barrier((first, wg, wu, wd))
    line = join(first)
    pieces = [line, swap(line, True, MIXED, 1), swap(line, True, MIXED, 2)]
    t_last = swap(line[:, :back_width], True, MIXED, 3)
    g_last = swap(line[:, back_width:], True, MIXED, 3)
    far_pieces = [swap_core(v) for v in pieces]
    t_near = join([v[:, :back_width] for v in pieces] + [t_last])
    t_far = join([v[:, :back_width] for v in far_pieces] + [swap_core(t_last)])
    half = t_near.shape[0]
    slots = 16 * CAP
    rows_in, act, gate_fac, up_fac, weighted, s_near, s_far = pl.pallas_call(
        forward_kernel,
        in_specs=[whole(pltpu.SMEM)] + [whole()] * 4,
        out_specs=[whole()] * 7,
        out_shape=[pltpu.VMEM((slots, width), BF16)]
        + [pltpu.VMEM((slots, hidden), F32)] * 3
        + [pltpu.VMEM((slots, hidden), BF16)]
        + [pltpu.VMEM((slots, half), BF16)] * 2,
        compiler_params=limit(16),
        cost_estimate=pl.CostEstimate(flops=1, transcendentals=0, bytes_accessed=1),
        name="forward",
    )(shard_of, in_vmem(t_near), in_vmem(t_far), wg, wu)
    g_last, _ = lax.optimization_barrier((g_last, s_near))
    g_near = join([v[:, back_width:] for v in pieces] + [g_last])
    g_far = join([v[:, back_width:] for v in far_pieces] + [swap_core(g_last)])
    ret_near, ret_far, rows_grad, gate_grad, up_grad = pl.pallas_call(
        backward_kernel,
        in_specs=[whole(pltpu.SMEM)] + [whole()] * 10,
        out_specs=[whole()] * 5,
        out_shape=[pltpu.VMEM((half, back_width), BF16)] * 2
        + [pltpu.VMEM((slots, width), BF16)]
        + [pltpu.VMEM((slots, hidden), BF16)] * 2,
        compiler_params=limit(16),
        name="backward",
    )(shard_of, in_vmem(g_near), in_vmem(g_far), s_near, s_far, act, gate_fac, up_fac, wg, wu, wd)
    peer = swap_core(ret_far)
    summed = (ret_near.astype(F32) + peer.astype(F32)).astype(BF16)
    got = fold(summed, True, MIXED)
    grad_gate, grad_up = weight_grads_of((gate_grad, rows_in), (up_grad, rows_in))
    got, grad_gate, grad_up = lax.optimization_barrier((got, grad_gate, grad_up))
    summed = sum(g.astype(F32) for g in got).astype(BF16)
    got = fold(summed, False, MIXED)
    (grad_down,) = weight_grads_of((weighted, rows_grad))
    got, grad_down = lax.optimization_barrier((got, grad_down))
    mine_input, mine_gates = pl.pallas_call(
        final_kernel,
        in_specs=[whole()] * 5,
        out_specs=[whole()] * 2,
        out_shape=[
            jax.ShapeDtypeStruct((rows, width), BF16),
            jax.ShapeDtypeStruct((rows, top_k), F32),
        ],
        compiler_params=limit(4),
        name="finish",
    )(*[in_vmem(g) for g in got], routes[0])
    return (
        mine_input[None],
        mine_gates[None],
        grad_gate[None, None],
        grad_up[None, None],
        grad_down[None, None],
    )


def mapped(local, mesh, group, expert):
    return jax.shard_map(
        local,
        mesh=mesh,
        in_specs=(
            P(expert, group, None),
            P(expert, group, None),
            P(expert, group, None),
            P(expert, group, None),
            P(),
            P(group, expert, None, None),
            P(group, expert, None, None),
            P(group, expert, None, None),
        ),
        out_specs=(
            P(expert, group, None),
            P(expert, group, None),
            P(group, expert, None, None),
            P(group, expert, None, None),
            P(group, expert, None, None),
        ),
        check_vma=False,
    )


def solution(mesh):
    if mesh.shape["group"] == 2 and mesh.shape["expert"] == 16:
        split = Mesh(mesh.devices.reshape(2, 4, 2, 2), ("x", "z", "y", "core"))
        return mapped(block_local, split, "x", ("z", "y", "core"))
    return mapped(general_local, mesh, "group", "expert")
```

```python
import functools

import jax
import jax.numpy as jnp
from jax import lax
from jax.experimental import pallas as pl
from jax.experimental.pallas import tpu as pltpu
from jax.sharding import Mesh
from jax.sharding import PartitionSpec as P

EXP_GROUP = 16
CAP = 8
LANES = 128
F32 = jnp.float32
BF16 = jnp.bfloat16


def expert_backward(rows_in, rows_grad, row_gates, gate_shard, up_shard, down_shard):
    contraction_dims = (((1,), (1,)), ((), ()))
    gate_pre = lax.dot_general(rows_in, gate_shard, contraction_dims, preferred_element_type=F32)
    up_pre = lax.dot_general(rows_in, up_shard, contraction_dims, preferred_element_type=F32)
    back_hidden = lax.dot_general(
        rows_grad, down_shard, contraction_dims, preferred_element_type=F32
    )
    sigmoid = jax.nn.sigmoid(gate_pre)
    swish_gate = gate_pre * sigmoid
    hidden = swish_gate * up_pre
    gate_part = jnp.sum(back_hidden * hidden, axis=1).astype(BF16)
    hidden_grad = row_gates[:, None] * back_hidden
    gate_grad = (hidden_grad * up_pre * sigmoid * (1.0 + gate_pre * (1.0 - sigmoid))).astype(BF16)
    up_grad = (hidden_grad * swish_gate).astype(BF16)
    input_part = (
        jnp.dot(gate_grad, gate_shard, preferred_element_type=F32)
        + jnp.dot(up_grad, up_shard, preferred_element_type=F32)
    ).astype(BF16)
    gate_weighted = (row_gates[:, None] * hidden).astype(BF16)
    return (input_part, gate_part, gate_grad, up_grad, gate_weighted)


def weight_grads(rows_in, rows_grad, gate_grad, up_grad, gate_weighted):
    contraction_dims = (((0,), (0,)), ((), ()))

    def one(a, b):
        return lax.dot_general(a, b, contraction_dims, preferred_element_type=F32).astype(BF16)

    return one(gate_grad, rows_in), one(up_grad, rows_in), one(gate_weighted, rows_grad)


def exchange(x):
    return lax.all_to_all(x, "expert", split_axis=0, concat_axis=0, tiled=True)


def general_local(tokens, out_grad, gates, routes, shard_of, w_gate, w_up, w_down):
    positions = lax.axis_size("expert")
    group_now = lax.axis_index("group")
    shards = positions // EXP_GROUP
    gather = functools.partial(lax.all_gather, axis_name="group", axis=1, tiled=True)
    all_in, all_grad, all_gates, all_ids = (
        gather(tokens),
        gather(out_grad),
        gather(gates),
        gather(routes),
    )
    width = tokens.shape[2]
    block_rows = all_in.shape[1]
    top_k = routes.shape[2]
    pair_total = block_rows * top_k
    bucket_total = EXP_GROUP * CAP
    local_ids = all_ids.reshape(pair_total) - group_now * EXP_GROUP
    onehot = (local_ids[:, None] == jnp.arange(EXP_GROUP, dtype=jnp.int32)[None, :]).astype(
        jnp.int32
    )
    slot_rank = jnp.sum((jnp.cumsum(onehot, axis=0) - 1) * onehot, axis=1)
    owned = (local_ids >= 0) & (local_ids < EXP_GROUP)
    target = jnp.where(owned, local_ids * CAP + slot_rank, bucket_total)
    pair_index = jnp.arange(pair_total, dtype=jnp.int32)
    slot_token = (
        jnp.full((bucket_total + 1,), block_rows, jnp.int32)
        .at[target]
        .set(pair_index // top_k)[:bucket_total]
    )
    slot_pair = (
        jnp.full((bucket_total + 1,), pair_total, jnp.int32)
        .at[target]
        .set(pair_index)[:bucket_total]
    )
    padded_in = jnp.concatenate([all_in[0], jnp.zeros((1, width), BF16)], axis=0)
    padded_grad = jnp.concatenate([all_grad[0], jnp.zeros((1, width), BF16)], axis=0)
    padded_gates = jnp.concatenate([all_gates.reshape(pair_total), jnp.zeros((1,), BF16)], axis=0)
    holder_expert = lax.dynamic_slice_in_dim(shard_of, group_now, 1, 0)[0] // shards
    send_token = slot_token.reshape(EXP_GROUP, CAP)[holder_expert]
    send_pair = slot_pair.reshape(EXP_GROUP, CAP)[holder_expert]
    rows_in = exchange(padded_in[send_token]).reshape(positions * CAP, width)
    rows_grad = exchange(padded_grad[send_token]).reshape(positions * CAP, width)
    row_gates = exchange(padded_gates[send_pair]).reshape(positions * CAP).astype(F32)
    input_part, gate_part, gate_grad, up_grad, gate_weighted = expert_backward(
        rows_in, rows_grad, row_gates, w_gate[0, 0], w_up[0, 0], w_down[0, 0]
    )
    grad_gate, grad_up, grad_down = weight_grads(
        rows_in, rows_grad, gate_grad, up_grad, gate_weighted
    )
    back_in = exchange(input_part.reshape(positions, CAP, width))
    back_gates = exchange(gate_part.reshape(positions, CAP))
    token_of_row = send_token.reshape(positions * CAP)
    pair_of_row = send_pair.reshape(positions * CAP)
    back_rows = back_in.reshape(positions * CAP, width).astype(F32)
    back_terms = back_gates.reshape(positions * CAP).astype(F32)
    block_input = (
        jnp.zeros((block_rows + 1, width), F32).at[token_of_row].add(back_rows)[:block_rows]
    )
    block_gates = jnp.zeros((pair_total + 1,), F32).at[pair_of_row].add(back_terms)[:pair_total]
    scatter = functools.partial(
        lax.psum_scatter, axis_name="group", scatter_dimension=1, tiled=True
    )
    mine_input = scatter(block_input[None])
    mine_gates = scatter(block_gates.reshape(1, block_rows, top_k))
    return (
        mine_input.astype(BF16),
        mine_gates,
        grad_gate[None, None],
        grad_up[None, None],
        grad_down[None, None],
    )


def dot_on(a, b, da, db):
    return lax.dot_general(a, b, (((da,), (db,)), ((), ())), preferred_element_type=F32)


def build_message(
    tok_hbm, grad_hbm, gates_hbm, routes_hbm, out_ref, tok_ref, grad_ref, gates_ref, routes_ref, sems
):
    width = tok_ref.shape[1]
    arrivals = (
        (gates_hbm, gates_ref), (routes_hbm, routes_ref), (tok_hbm, tok_ref), (grad_hbm, grad_ref),
    )
    copies = [pltpu.make_async_copy(*pair, sems.at[n]) for n, pair in enumerate(arrivals)]
    for copy in copies:
        copy.start()
    for copy in copies:
        copy.wait()
    out_ref[:, :width] = tok_ref[...]
    out_ref[:, width + LANES :] = grad_ref[...]
    rows, top_k = routes_ref.shape
    lane = lax.broadcasted_iota(jnp.int32, (rows, LANES), 1)
    routes = routes_ref[...]
    gates = gates_ref[...].astype(F32)
    dense = jnp.zeros((rows, LANES), F32)
    for k in range(top_k):
        chosen = routes[:, k : k + 1]
        dense = jnp.where(lane == chosen, gates[:, k : k + 1], dense)
        dense = jnp.where(lane == chosen + LANES // 2, 1.0, dense)
    out_ref[:, width : width + LANES] = dense.astype(BF16)


def my_expert(shard_ref):
    group = lax.axis_index("x")
    place = (lax.axis_index("z") * 2 + lax.axis_index("y")) * 2 + lax.axis_index("core")
    return shard_ref[group, place] + group * EXP_GROUP


def load(src_ref, dst_ref, sems, parts=4):
    step = src_ref.shape[0] // parts
    copies = []
    for i in range(parts):
        part = slice(i * step, (i + 1) * step)
        copies.append(pltpu.make_async_copy(src_ref.at[part], dst_ref.at[part], sems.at[i]))
        copies[-1].start()
    return copies


def prefetch_kernel(*refs):
    count = (len(refs) - 1) // 2
    sems = refs[-1]
    copies = []
    for n in range(count):
        copies += load(refs[n], refs[count + n], sems.at[n])
    for copy in copies:
        copy.wait()


def prefetch(*weights):
    return pl.pallas_call(
        prefetch_kernel,
        in_specs=[whole(pltpu.HBM)] * len(weights),
        out_specs=[whole()] * len(weights),
        out_shape=[pltpu.VMEM(w.shape, w.dtype) for w in weights],
        scratch_shapes=[pltpu.SemaphoreType.DMA((len(weights), 4))],
        compiler_params=limit(2),
        name="prefetch",
    )(*(in_hbm(w) for w in weights))


def forward_kernel(
    shard_ref, near_ref, far_ref, wg_ref, wu_ref,
    rin_ref, hidden_ref, gfac_ref, ufac_ref, gw_ref, select_ref,
):
    which = my_expert(shard_ref)
    half = near_ref.shape[0]
    slots, width = rin_ref.shape
    total = 2 * half
    lane = lax.broadcasted_iota(jnp.int32, (8, LANES), 1)
    pick_gate = jnp.where(lane == which, 1.0, 0.0).astype(BF16)
    pick_mask = jnp.where(lane == which + LANES // 2, 1.0, 0.0).astype(BF16)
    extra = jnp.concatenate([near_ref[:, width:], far_ref[:, width:]], axis=0)
    gate_row = dot_on(pick_gate, extra, 1, 1)
    mask_row = dot_on(pick_mask, extra, 1, 1)
    before = (
        lax.broadcasted_iota(jnp.int32, (total, total), 0)
        < lax.broadcasted_iota(jnp.int32, (total, total), 1)
    )
    before = jnp.where(before, 1.0, 0.0).astype(BF16)
    rank_row = dot_on(mask_row.astype(BF16), before, 1, 0)
    slot = lax.broadcasted_iota(jnp.int32, (slots, total), 0)
    hit = (slot == rank_row[:1].astype(jnp.int32)) & (mask_row[:1] > 0.5)
    select_f = jnp.where(hit, 1.0, 0.0)
    select = select_f.astype(BF16)
    row_gates = jnp.sum(select_f * gate_row[:1], axis=1, keepdims=True)
    both = jnp.concatenate([near_ref[:, :width], far_ref[:, :width]], axis=0)
    rows_in = dot_on(select, both, 1, 0).astype(BF16)
    rin_ref[...] = rows_in
    select_ref[...] = select
    gate_pre = dot_on(rows_in, wg_ref[...], 1, 1)
    up_pre = dot_on(rows_in, wu_ref[...], 1, 1)
    sigmoid = jax.nn.sigmoid(gate_pre)
    swish_gate = gate_pre * sigmoid
    hidden = swish_gate * up_pre
    hidden_ref[...] = hidden
    gw_ref[...] = (row_gates * hidden).astype(BF16)
    ufac_ref[...] = row_gates * swish_gate
    gfac_ref[...] = row_gates * (up_pre * sigmoid * (1.0 + gate_pre * (1.0 - sigmoid)))


def backward_kernel(
    shard_ref, near_ref, far_ref, last_ref, select_ref, hidden_ref, gfac_ref, ufac_ref,
    wg_ref, wu_ref, wd_ref,
    ret_near_ref, ret_far_ref, rgrad_ref, gg_ref, ug_ref,
):
    which = my_expert(shard_ref)
    slots, width = rgrad_ref.shape
    select = select_ref[...]
    half = near_ref.shape[0]
    both = jnp.concatenate([near_ref[...], far_ref[...], last_ref[...]], axis=0)
    rows_grad = dot_on(select, both, 1, 0).astype(BF16)
    rgrad_ref[...] = rows_grad
    back = dot_on(rows_grad, wd_ref[...], 1, 1)
    gate_grad = (back * gfac_ref[...]).astype(BF16)
    up_grad = (back * ufac_ref[...]).astype(BF16)
    gg_ref[...] = gate_grad
    ug_ref[...] = up_grad
    gate_part = jnp.sum(back * hidden_ref[...], axis=1, keepdims=True)
    input_part = (
        dot_on(gate_grad, wg_ref[...], 1, 0) + dot_on(up_grad, wu_ref[...], 1, 0)
    ).astype(BF16)
    gate_lane = lax.broadcasted_iota(jnp.int32, (slots, LANES), 1)
    gate_cols = jnp.where(gate_lane == which, gate_part, 0.0).astype(BF16)
    terms = jnp.concatenate([input_part, gate_cols], axis=1)
    ret_far_ref[...] = dot_on(select[:, half:], terms, 0, 0).astype(BF16)
    ret_near_ref[...] = dot_on(select[:, :half], terms, 0, 0).astype(BF16)


def weight_kernel(tile, count, *refs):
    pairs = [(refs[2 * n], refs[2 * n + 1]) for n in range(count)]
    outs = refs[2 * count : 3 * count]
    held, sems = refs[3 * count :]
    steps = outs[0].shape[0] // tile
    copies = []
    for n, ((a_ref, b_ref), out) in enumerate(zip(pairs, outs)):
        for i in range(steps):
            part = slice(i * tile, (i + 1) * tile)
            held[n, part, :] = dot_on(a_ref[:, part], b_ref[...], 0, 0).astype(BF16)
            copy = pltpu.make_async_copy(held.at[n, part, :], out.at[part, :], sems.at[n, i])
            copy.start()
            copies.append(copy)
    for copy in copies:
        copy.wait()


def weight_grads_of(*pairs, tile=256):
    count = len(pairs)
    hidden = pairs[0][0].shape[1]
    width = pairs[0][1].shape[1]
    flat = [in_vmem(v) for pair in pairs for v in pair]
    return pl.pallas_call(
        functools.partial(weight_kernel, tile, count),
        in_specs=[whole()] * len(flat),
        out_specs=[whole(pl.ANY)] * count,
        out_shape=[jax.ShapeDtypeStruct((hidden, width), BF16)] * count,
        scratch_shapes=[
            pltpu.VMEM((count, hidden, width), BF16),
            pltpu.SemaphoreType.DMA((count, hidden // tile)),
        ],
        compiler_params=limit(3 + 4 * count),
        name="weight_grads",
    )(*flat)


def sum_kernel(a_ref, b_ref, c_ref, d_ref, out_ref):
    out_ref[...] = (
        a_ref[...].astype(F32) + b_ref[...].astype(F32) + c_ref[...].astype(F32)
        + d_ref[...].astype(F32)
    ).astype(BF16)


def final_kernel(a_ref, b_ref, c_ref, d_ref, routes_ref, in_ref, gate_ref):
    total = (
        a_ref[...].astype(F32) + b_ref[...].astype(F32) + c_ref[...].astype(F32)
        + d_ref[...].astype(F32)
    )
    width = in_ref.shape[1]
    in_ref[...] = total[:, :width].astype(BF16)
    dense = total[:, width:]
    rows, top_k = routes_ref.shape
    routes = routes_ref[...]
    lane = lax.broadcasted_iota(jnp.int32, dense.shape, 1)
    place = lax.broadcasted_iota(jnp.int32, (rows, top_k), 1)
    out = jnp.zeros((rows, top_k), F32)
    for k in range(top_k):
        value = jnp.sum(jnp.where(lane == routes[:, k : k + 1], dense, 0.0), axis=1, keepdims=True)
        out = jnp.where(place == k, value, out)
    gate_ref[...] = out


MIXED = True
AXES = ("x", "z", "y", "core")


def limit(mebibytes):
    return pltpu.CompilerParams(vmem_limit_bytes=mebibytes * 1024 * 1024)


def whole(memory=pltpu.VMEM):
    return pl.BlockSpec(memory_space=memory)


def in_vmem(x):
    return pltpu.with_memory_space_constraint(x, pltpu.VMEM)


def in_hbm(x):
    return pltpu.with_memory_space_constraint(x, pltpu.HBM)


def partner(device, plane, k):
    x, z, y, core = device // 16, device // 4 % 4, device // 2 % 2, device % 2
    if plane:
        x, y = x ^ (k & 1), y ^ (k >> 1)
    else:
        z = z ^ k
    return ((x * 4 + z) * 2 + y) * 2 + core


def swap(value, late, mixed, k):
    pairs = []
    for device in range(32):
        plane = late != (mixed and device % 2 == 1)
        pairs.append((device, partner(device, plane, k)))
    return lax.ppermute(value, AXES, pairs)


def swap_core(value):
    return lax.ppermute(value, AXES, [(d, d ^ 1) for d in range(32)])


def spread(value, late, mixed):
    return [value] + [swap(value, late, mixed, k) for k in (1, 2, 3)]


def join(pieces):
    return jnp.concatenate(pieces, axis=0)


def fold(value, late, mixed):
    part = value.shape[0] // 4
    pieces = [value[k * part : (k + 1) * part] for k in range(4)]
    return [pieces[0]] + [swap(pieces[k], late, mixed, k) for k in (1, 2, 3)]


def block_local(tokens, out_grad, gates, routes, shard_of, w_gate, w_up, w_down):
    width = tokens.shape[2]
    rows = tokens.shape[1]
    hidden = w_gate.shape[2]
    top_k = routes.shape[2]
    back_width = width + LANES
    message = pl.pallas_call(
        build_message,
        in_specs=[whole(pltpu.HBM)] * 4,
        out_specs=whole(),
        scratch_shapes=[
            pltpu.VMEM(v.shape[1:], v.dtype) for v in (tokens, out_grad, gates, routes)
        ]
        + [pltpu.SemaphoreType.DMA((4,))],
        out_shape=pltpu.VMEM((rows, back_width + width), BF16),
        compiler_params=limit(4),
        name="build_message",
    )(*(in_hbm(v[0]) for v in (tokens, out_grad, gates, routes)))
    first = spread(message, False, MIXED)
    wg, wu, wd = prefetch(w_gate[0, 0], w_up[0, 0], w_down[0, 0])
    first, wg, wu, wd = lax.optimization_barrier((first, wg, wu, wd))
    line = join(first)
    pieces = [line, swap(line, True, MIXED, 1), swap(line, True, MIXED, 2)]
    t_last = swap(line[:, :back_width], True, MIXED, 3)
    g_last = swap(line[:, back_width:], True, MIXED, 3)
    far_pieces = [swap_core(v) for v in pieces]
    t_near = join([v[:, :back_width] for v in pieces] + [t_last])
    t_far = join([v[:, :back_width] for v in far_pieces] + [swap_core(t_last)])
    g_far = join([v[:, back_width:] for v in far_pieces])
    g_last, g_far, _ = lax.optimization_barrier((g_last, g_far, t_far))
    g_near = join([v[:, back_width:] for v in pieces] + [g_last])
    g_far_last = swap_core(g_last)
    half = t_near.shape[0]
    slots = 16 * CAP
    rows_in, act, gate_fac, up_fac, weighted, select = pl.pallas_call(
        forward_kernel,
        in_specs=[whole(pltpu.SMEM)] + [whole()] * 4,
        out_specs=[whole()] * 6,
        out_shape=[pltpu.VMEM((slots, width), BF16)]
        + [pltpu.VMEM((slots, hidden), F32)] * 3
        + [pltpu.VMEM((slots, hidden), BF16)]
        + [pltpu.VMEM((slots, 2 * half), BF16)],
        compiler_params=limit(8),
        cost_estimate=pl.CostEstimate(flops=1, transcendentals=0, bytes_accessed=1),
        name="forward",
    )(shard_of, in_vmem(t_near), in_vmem(t_far), wg, wu)
    ret_near, ret_far, rows_grad, gate_grad, up_grad = pl.pallas_call(
        backward_kernel,
        in_specs=[whole(pltpu.SMEM)] + [whole()] * 10,
        out_specs=[whole()] * 5,
        out_shape=[pltpu.VMEM((half, back_width), BF16)] * 2
        + [pltpu.VMEM((slots, width), BF16)]
        + [pltpu.VMEM((slots, hidden), BF16)] * 2,
        compiler_params=limit(8),
        name="backward",
    )(shard_of, in_vmem(g_near), in_vmem(g_far), in_vmem(g_far_last), select, act, gate_fac, up_fac, wg, wu, wd)
    peer = swap_core(ret_far)
    summed = (ret_near.astype(F32) + peer.astype(F32)).astype(BF16)
    got = fold(summed, True, MIXED)
    grad_gate, grad_up = weight_grads_of((gate_grad, rows_in), (up_grad, rows_in))
    got, grad_gate, grad_up = lax.optimization_barrier((got, grad_gate, grad_up))
    summed = sum(g.astype(F32) for g in got).astype(BF16)
    got = fold(summed, False, MIXED)
    (grad_down,) = weight_grads_of((weighted, rows_grad))
    got, grad_down = lax.optimization_barrier((got, grad_down))
    mine_input, mine_gates = pl.pallas_call(
        final_kernel,
        in_specs=[whole()] * 5,
        out_specs=[whole()] * 2,
        out_shape=[
            jax.ShapeDtypeStruct((rows, width), BF16),
            jax.ShapeDtypeStruct((rows, top_k), F32),
        ],
        compiler_params=limit(4),
        name="finish",
    )(*[in_vmem(g) for g in got], routes[0])
    return (
        mine_input[None],
        mine_gates[None],
        grad_gate[None, None],
        grad_up[None, None],
        grad_down[None, None],
    )


def mapped(local, mesh, group, expert):
    return jax.shard_map(
        local,
        mesh=mesh,
        in_specs=(
            P(expert, group, None),
            P(expert, group, None),
            P(expert, group, None),
            P(expert, group, None),
            P(),
            P(group, expert, None, None),
            P(group, expert, None, None),
            P(group, expert, None, None),
        ),
        out_specs=(
            P(expert, group, None),
            P(expert, group, None),
            P(group, expert, None, None),
            P(group, expert, None, None),
            P(group, expert, None, None),
        ),
        check_vma=False,
    )


def solution(mesh):
    if mesh.shape["group"] == 2 and mesh.shape["expert"] == 16:
        split = Mesh(mesh.devices.reshape(2, 4, 2, 2), ("x", "z", "y", "core"))
        return mapped(block_local, split, "x", ("z", "y", "core"))
    return mapped(general_local, mesh, "group", "expert")
```
